256 devices in a mesh: ctx: 16 (over y, x), head: 4 (over z_lo, core), clip: 4 (over z_hi).
Axes of the slice: x: 4, y: 4, z: 8 (z_hi: 4, z_lo: 2; z = z_hi * 2 + z_lo), core: 2. Of those that a mesh axis runs over, the one named last changes fastest.
Arguments:
- queries: bfloat16 [4, 2048, 2560], P('clip', 'ctx', 'head'), may hold values from -40 to 40
- key_states: bfloat16 [4, 2048, 2560], P('clip', 'ctx', 'head'), may hold values from -40 to 40
- value_states: bfloat16 [4, 2048, 2560], P('clip', 'ctx', 'head'), may hold values from -40 to 40
- layer_grad: bfloat16 [4, 2048, 5120], P('clip', 'ctx'), may hold values from -6 to 6
- out_weight: bfloat16 [2560, 5120], P('head', 'clip'), may hold values from -0.125 to 0.125
- chosen: int32 [4, 32, 4], P('clip', 'ctx'), may hold values from 0 to 31, all different within a row
Outputs:
- attention: bfloat16 [4, 2048, 2560], P('clip', 'ctx', 'head')
- query_grad: bfloat16 [4, 2048, 2560], P('clip', 'ctx', 'head')
- key_grad: bfloat16 [4, 2048, 2560], P('clip', 'ctx', 'head')
- value_grad: bfloat16 [4, 2048, 2560], P('clip', 'ctx', 'head')
- weight_grad: bfloat16 [2560, 5120], P('head', 'clip')
The draws below stay inside these ranges and needn't reach their ends.
Inputs may be any that keep to these rules, and one draw needn't show every extreme that they name: Each row names 4 different cubes of its clip; how often a key cube is chosen differs widely from cube to cube.
All inputs are finite; a program needn't handle non-finite values.
Results may differ from the reference program's by a relative error of at most 0.025.
Values may be sent and summed in bfloat16 or wider, within the bound.
No kernel may reach another device: no remote copies, remote signals or barrier semaphores. Data moves between devices by JAX's collectives and lax.ppermute only.
A program may use at most 128 MiB of HBM per device.

```python
import jax
import jax.numpy as jnp
from jax import lax

D = 5120
HD = 128
CUBE = 64
CUBES_DEV = 2
HEADS = 20
NC = 32
TOKENS = 2048
TOPK = 4
CLIPS = 4
N_CTX = 16


def cube_field(key, salt):
    field = jax.random.normal(jax.random.fold_in(key, salt), (CLIPS, NC, 1, HEADS * HD), jnp.float32)
    return jnp.broadcast_to(field, (CLIPS, NC, CUBE, HEADS * HD)).reshape(CLIPS, TOKENS, HEADS * HD)


def draw_queries(key, part):
    noise_key = jax.random.fold_in(key, 1)
    drawn = jax.random.normal(noise_key, (CLIPS, TOKENS, HEADS * HD), jnp.float32) + cube_field(key, 211)
    return jnp.clip(drawn, -40.0, 40.0).astype(jnp.bfloat16)


def draw_key_states(key, part):
    noise_key = jax.random.fold_in(key, 2)
    drawn = jax.random.normal(noise_key, (CLIPS, TOKENS, HEADS * HD), jnp.float32) + cube_field(key, 223)
    return jnp.clip(drawn, -40.0, 40.0).astype(jnp.bfloat16)


def draw_value_states(key, part):
    noise_key = jax.random.fold_in(key, 4)
    drawn = jax.random.normal(noise_key, (CLIPS, TOKENS, HEADS * HD), jnp.float32) + cube_field(key, 227)
    return jnp.clip(drawn, -40.0, 40.0).astype(jnp.bfloat16)


def shard_levels(key, shape, cuts, least, high):
    def one(axis_at, shards_of):
        heights = jax.random.uniform(jax.random.fold_in(jax.random.fold_in(key, 6), axis_at), (shards_of,), jnp.float32, least / len(cuts), high / len(cuts))
        return jnp.repeat(jnp.exp(heights), shape[axis_at] // shards_of).reshape((-1,) + (1,) * (len(shape) - axis_at - 1))

    loudness = one(*cuts[0])
    for cut in cuts[1:]:
        loudness = loudness * one(*cut)
    return loudness


def picks_of(stream_key, rows, number_of, top, lift):
    ranking = jax.random.permutation(jax.random.fold_in(stream_key, 1), number_of)
    boost = ranking
    for power in range(3):
        boost = boost * boost // number_of
    boost = boost * lift // number_of
    chance = jax.random.randint(jax.random.fold_in(stream_key, 2), (rows, number_of), 0, 4096) + boost
    holders = jax.random.permutation(jax.random.fold_in(stream_key, 3), rows)[jnp.arange(number_of) % rows]
    chance = jnp.where(jnp.arange(rows)[:, None] == holders[None, :], 1 << 14, chance)
    priority = chance * number_of + jnp.arange(number_of)
    return lax.top_k(priority.astype(jnp.int32), top)[1].astype(jnp.int32)


def normal_values(own_key, extent, spread, reach, pieces=(), held_as=jnp.bfloat16):
    result = spread * jax.random.normal(own_key, extent, jnp.float32)
    if pieces:
        result = result * shard_levels(own_key, extent, pieces, -0.22, 0.18)
    return jnp.clip(result, -reach, reach).astype(held_as)


def setup_inputs(seed: int = 0) -> dict:
    splits = jax.random.split(jax.random.key(seed), 7)
    return {
        "queries": draw_queries(jax.random.fold_in(splits[6], 71), 0),
        "key_states": draw_key_states(jax.random.fold_in(splits[6], 71), 0),
        "value_states": draw_value_states(jax.random.fold_in(splits[6], 71), 0),
        "layer_grad": normal_values(splits[3], (CLIPS, TOKENS, D), 1.0, 6.0, ((0, 4), (1, 16))),
        "out_weight": normal_values(splits[4], (HEADS * HD, D), (HEADS * HD) ** -0.5, 0.125, ((0, 4), (1, 4))),
        "chosen": picks_of(splits[5], CLIPS * NC, NC, TOPK, 2048).reshape((CLIPS, NC, TOPK)),
    }


def pooled(blocks):
    grouped = blocks.astype(jnp.float32).reshape(-1, CUBE, blocks.shape[-1])
    return jnp.mean(grouped, axis=1).astype(jnp.bfloat16)


def softmax_rows(scores):
    largest = jnp.max(scores, axis=-1, keepdims=True)
    expons = jnp.exp(scores - largest)
    return expons / jnp.sum(expons, axis=-1, keepdims=True)


def group_sum(picked_terms, coarse_weights, coarse_inputs, chosen_group):
    running = jnp.zeros((NC, CUBE, HD), jnp.float32)
    running = running.at[chosen_group.reshape(-1)].add(picked_terms.reshape(-1, CUBE, HD))
    cube_term = jnp.dot(coarse_weights.T.astype(jnp.float32), coarse_inputs.astype(jnp.float32))
    rounded = lax.optimization_barrier((running + cube_term[:, None, :] / CUBE).astype(jnp.bfloat16))
    return rounded.astype(jnp.float32)


def one_head(inputs):
    query_rows, key_rows, value_rows, grad_rows, chosen_rows = inputs
    scaling = HD ** -0.5
    q_cube = pooled(query_rows)
    k_cube = pooled(key_rows)
    v_cube = pooled(value_rows)
    coarse_p = softmax_rows(jnp.dot(q_cube, k_cube.T, preferred_element_type=jnp.float32) * scaling)
    coarse_half = coarse_p.astype(jnp.bfloat16)
    coarse_out = jnp.dot(coarse_half, v_cube, preferred_element_type=jnp.float32)
    query_blocks = query_rows.reshape(NC, CUBE, HD).astype(jnp.float32)
    grad_blocks = grad_rows.reshape(NC, CUBE, HD).astype(jnp.float32)
    key_pick = key_rows.reshape(NC, CUBE, HD)[chosen_rows].reshape(NC, TOPK * CUBE, HD).astype(jnp.float32)
    value_pick = value_rows.reshape(NC, CUBE, HD)[chosen_rows].reshape(NC, TOPK * CUBE, HD).astype(jnp.float32)
    fine_p = softmax_rows(jnp.einsum("ctd,ckd->ctk", query_blocks, key_pick) * scaling)
    fine_half = fine_p.astype(jnp.bfloat16)
    fine_out = jnp.einsum("ctk,ckd->ctd", fine_half.astype(jnp.float32), value_pick)
    attention = (fine_out + coarse_out[:, None, :]).astype(jnp.bfloat16).reshape(TOKENS, HD)
    grad_cube = jnp.sum(grad_blocks, axis=1).astype(jnp.bfloat16)
    coarse_dp = jnp.dot(grad_cube, v_cube.T, preferred_element_type=jnp.float32)
    coarse_delta = jnp.sum(coarse_p * coarse_dp, axis=-1, keepdims=True)
    coarse_ds = (scaling * coarse_p * (coarse_dp - coarse_delta)).astype(jnp.bfloat16)
    coarse_dq = jnp.dot(coarse_ds, k_cube, preferred_element_type=jnp.float32)
    fine_dp = jnp.einsum("ctd,ckd->ctk", grad_blocks, value_pick)
    fine_delta = jnp.sum(fine_p * fine_dp, axis=-1, keepdims=True)
    fine_ds = (scaling * fine_p * (fine_dp - fine_delta)).astype(jnp.bfloat16)
    query_grad = jnp.einsum("ctk,ckd->ctd", fine_ds.astype(jnp.float32), key_pick) + coarse_dq[:, None, :] / CUBE
    query_grad = query_grad.astype(jnp.bfloat16).reshape(TOKENS, HD)
    key_picked = jnp.einsum("ctk,ctd->ckd", fine_ds.astype(jnp.float32), query_blocks)
    value_picked = jnp.einsum("ctk,ctd->ckd", fine_half.astype(jnp.float32), grad_blocks)
    key_picked = key_picked.reshape(N_CTX, CUBES_DEV, TOPK, CUBE, HD)
    value_picked = value_picked.reshape(N_CTX, CUBES_DEV, TOPK, CUBE, HD)
    chosen_groups = chosen_rows.reshape(N_CTX, CUBES_DEV, TOPK)
    key_terms = jax.vmap(group_sum)(key_picked, coarse_ds.reshape(N_CTX, CUBES_DEV, NC),
                                    q_cube.reshape(N_CTX, CUBES_DEV, HD), chosen_groups)
    value_terms = jax.vmap(group_sum)(value_picked, coarse_half.reshape(N_CTX, CUBES_DEV, NC),
                                      grad_cube.reshape(N_CTX, CUBES_DEV, HD), chosen_groups)
    key_grad = jnp.sum(key_terms, axis=0).astype(jnp.bfloat16).reshape(TOKENS, HD)
    value_grad = jnp.sum(value_terms, axis=0).astype(jnp.bfloat16).reshape(TOKENS, HD)
    return attention, query_grad, key_grad, value_grad


def heads_first(tensor):
    return tensor.reshape(CLIPS, TOKENS, HEADS, HD).transpose(0, 2, 1, 3).reshape(CLIPS * HEADS, TOKENS, HD)


def heads_back(tensor):
    return tensor.reshape(CLIPS, HEADS, TOKENS, HD).transpose(0, 2, 1, 3).reshape(CLIPS, TOKENS, HEADS * HD)


def reference(queries, key_states, value_states, layer_grad, out_weight, chosen):
    grads_list = []
    for clip_index in range(CLIPS):
        grads_list.append(jnp.dot(layer_grad[clip_index], out_weight.T, preferred_element_type=jnp.float32))
    attn_grad = jnp.stack(grads_list).astype(jnp.bfloat16)
    chosen_heads = jnp.repeat(chosen, HEADS, axis=0)
    results = lax.map(one_head, (heads_first(queries), heads_first(key_states), heads_first(value_states),
                                 heads_first(attn_grad), chosen_heads))
    attention = heads_back(results[0])
    query_grad = heads_back(results[1])
    key_grad = heads_back(results[2])
    value_grad = heads_back(results[3])
    attn_groups = attention.reshape(CLIPS, N_CTX, CUBES_DEV * CUBE, HEADS * HD)
    layer_groups = layer_grad.reshape(CLIPS, N_CTX, CUBES_DEV * CUBE, D)

    def group_weight(running, group_index):
        clip_sum = jnp.zeros((HEADS * HD, D), jnp.float32)
        for clip_index in range(CLIPS):
            term = jnp.dot(attn_groups[clip_index, group_index].T, layer_groups[clip_index, group_index],
                           preferred_element_type=jnp.float32)
            clip_sum = clip_sum + lax.optimization_barrier(term.astype(jnp.bfloat16)).astype(jnp.float32)
        rounded = lax.optimization_barrier(clip_sum.astype(jnp.bfloat16)).astype(jnp.float32)
        return running + rounded, None

    weight_sum, _ = lax.scan(group_weight, jnp.zeros((HEADS * HD, D), jnp.float32),
                             jnp.arange(N_CTX, dtype=jnp.int32))
    return attention, query_grad, key_grad, value_grad, weight_sum.astype(jnp.bfloat16)
```

```python
import functools

import jax
import jax.numpy as jnp
from jax import lax
from jax.experimental import pallas as pl
from jax.experimental.pallas import tpu as pltpu
from jax.sharding import PartitionSpec as P

HD = 128
CUBE = 64
SIDE = 4
OFFS = (0, -1, 1, 2)
STAT = 16
F32 = jnp.float32
BF16 = jnp.bfloat16
NT = (((1,), (1,)), ((), ()))
NN = (((1,), (0,)), ((), ()))


def dot(a, b, dims=NN):
    return lax.dot_general(a, b, dims, preferred_element_type=F32)


def shift(v, along, by):
    pairs = []
    for y in range(SIDE):
        for x in range(SIDE):
            to = y * SIDE + (x + by) % SIDE if along == "x" else (y + by) % SIDE * SIDE + x
            pairs.append((y * SIDE + x, to))
    return lax.ppermute(v, "ctx", pairs)


def ring(v, along):
    n = v.shape[0]
    cut = n // 2 // 8 * 8
    low = shift(v, along, 1)
    high = shift(v, along, -1)
    return v, low, high, shift(low[:cut], along, 1), shift(high[cut:], along, -1)


def spread(v, first):
    n, w = v.shape
    row = jnp.concatenate(ring(v, first), axis=0)
    parts = ring(row, "y" if first == "x" else "x")
    return [part.reshape(-1, n, w) for part in parts]


def block_of(refs, place):
    if place < 12:
        return refs[place // 4], place % 4
    return refs[3 + (place - 12) // 2], place % 2


def whole(ref, at, cols):
    return ref[at, :, cols]


def pool_matrix(rows, tokens, base):
    r = lax.broadcasted_iota(jnp.int32, (rows, tokens), 0)
    t = lax.broadcasted_iota(jnp.int32, (rows, tokens), 1)
    lo = (r - base) * CUBE
    return jnp.where((t >= lo) & (t < lo + CUBE), 1.0, 0.0).astype(BF16)


def place_of(delta):
    d = jnp.where(delta < 0, delta + SIDE, delta)
    return jnp.where(d < 2, 2 * d, 7 - 2 * d)


def softmax_parts(s, axis):
    m = jnp.max(s, axis=axis, keepdims=True)
    e = jnp.exp(s - m)
    total = jnp.sum(e, axis=axis, keepdims=True)
    return e / total, m, total


def pieces_of(v):
    a = v.astype(BF16)
    rest = v - a.astype(F32)
    b = rest.astype(BF16)
    return a, b, (rest - b.astype(F32)).astype(BF16)


def query_kernel(scale, meta, q_ref, g0, g1, g2, g3, *rest):
    k_in, v_in = rest[:5], rest[5:10]
    att_ref, dq_ref, da_ref, db_ref, kc_ref, vc_ref, kall, vall, dall = rest[10:]
    heads = q_ref.shape[1] // HD
    tokens = q_ref.shape[0]
    for src, dst in ((k_in, kall), (v_in, vall)):
        at = 0
        for ref in src:
            cubes = 2 * ref.shape[0]
            for b in range(ref.shape[0]):
                dst[at + 2 * b] = ref[b, :CUBE]
                dst[at + 2 * b + 1] = ref[b, CUBE:]
            at += cubes
    summed = g0[...] + g1[...].astype(F32) + g2[...].astype(F32) + g3[...].astype(F32)
    dall[...] = summed.astype(BF16)
    grad = dall[...]
    da_ref[...] = grad[:CUBE]
    db_ref[:CUBE] = grad[CUBE:]
    pool8 = pool_matrix(8, 8 * CUBE, 0)
    i0 = lax.broadcasted_iota(jnp.int32, (32, 32), 0)
    i1 = lax.broadcasted_iota(jnp.int32, (32, 32), 1)
    partner = ((i0 // 2) % 4) * 8 + (i0 // 8) * 2 + i0 % 2
    swap = jnp.where(i1 == partner, 1.0, 0.0).astype(BF16)

    def means(src):
        rows = [
            dot(pool8, src[8 * p : 8 * p + 8].reshape(8 * CUBE, heads * HD)) for p in range(4)
        ]
        return (jnp.concatenate(rows, axis=0) * (1.0 / CUBE)).astype(BF16)

    kc = means(kall)
    vc = dot(swap, means(vall)).astype(BF16)
    kc_ref[...] = kc
    vc_ref[...] = vc
    pool2 = pool_matrix(8, tokens, 0)
    qc = (dot(pool2, q_ref[...]) * (1.0 / CUBE)).astype(BF16)
    gc = dot(pool2, grad).astype(BF16)
    eye = lax.broadcasted_iota(jnp.int32, (CUBE, HD), 0)
    lane = lax.broadcasted_iota(jnp.int32, (CUBE, HD), 1)
    y, x = meta[8], meta[9]
    kslot, vslot = [], []
    for c in range(2):
        for j in range(4):
            cube = meta[4 * c + j]
            dev = cube // 2
            py = place_of(dev // SIDE - y)
            px = place_of(dev % SIDE - x)
            kslot.append((py * 4 + px) * 2 + cube % 2)
            vslot.append((px * 4 + py) * 2 + cube % 2)
    for h in range(heads):
        cols = slice(h * HD, h * HD + HD)
        cp, _, _ = softmax_parts(dot(qc[:, cols], kc[:, cols], NT) * scale, 1)
        cout = dot(cp.astype(BF16), vc[:, cols])
        cdp = dot(gc[:, cols], vc[:, cols], NT)
        cds = (scale * cp * (cdp - jnp.sum(cp * cdp, axis=1, keepdims=True))).astype(BF16)
        cdq = dot(cds, kc[:, cols]) * (1.0 / CUBE)
        rows = [jnp.zeros((1, HD), F32) for _ in range(3)]
        for c in range(2):
            toks = slice(c * CUBE, c * CUBE + CUBE)
            k = jnp.concatenate([kall[kslot[4 * c + j], :, cols] for j in range(4)], axis=0)
            v = jnp.concatenate([vall[vslot[4 * c + j], :, cols] for j in range(4)], axis=0)
            q = q_ref[toks, cols]
            g = dall[toks, cols]
            p, m, total = softmax_parts(dot(q, k, NT) * scale, 1)
            out = dot(p.astype(BF16), v) + cout[c : c + 1]
            att_ref[toks, cols] = out.astype(BF16)
            dp = dot(g, v, NT)
            delta = jnp.sum(p * dp, axis=1, keepdims=True)
            ds = (scale * p * (dp - delta)).astype(BF16)
            dq_ref[toks, cols] = (dot(ds, k) + cdq[c : c + 1]).astype(BF16)
            on = lane == eye + c * CUBE
            rows = [
                r + jnp.sum(jnp.where(on, val, 0.0), axis=0, keepdims=True)
                for r, val in zip(rows, (m, total, delta))
            ]
        for n, r in enumerate(rows):
            for e, piece in enumerate(pieces_of(r)):
                db_ref[CUBE + 3 * n + e : CUBE + 3 * n + e + 1, cols] = piece
    lane1 = lax.broadcasted_iota(jnp.int32, (1, HD), 1)
    for j in range(4):
        pick = jnp.where(lane1 < CUBE, meta[j], meta[4 + j]).astype(F32).astype(BF16)
        for h in range(heads):
            db_ref[CUBE + 9 + j : CUBE + 10 + j, h * HD : h * HD + HD] = pick
    db_ref[CUBE + 13 :] = jnp.zeros((STAT - 13, heads * HD), BF16)


def key_kernel(scale, meta, q_ref, k_ref, v_ref, kc_ref, vc_ref, *rest):
    a_in, b_in = rest[:5], rest[5:10]
    dk_ref, dv_ref = rest[10:]
    heads = k_ref.shape[1] // HD
    y, x = meta[8], meta[9]
    cube0 = (2 * (y * SIDE + x)).astype(F32)
    for h in range(heads):
        cols = slice(h * HD, h * HD + HD)
        k, v = k_ref[:, cols], v_ref[:, cols]
        dk = jnp.zeros((2 * CUBE, HD), F32)
        dv = jnp.zeros((2 * CUBE, HD), F32)
        qsum = jnp.zeros((32, HD), F32)
        gsum = jnp.zeros((32, HD), F32)
        for py in range(4):
            qs, gs, stats = [], [], []
            for px in range(4):
                dev = lax.rem(y + OFFS[py] + SIDE, SIDE) * SIDE + lax.rem(x + OFFS[px] + SIDE, SIDE)
                qs.append(q_ref[dev, :, cols])
                ref, at = block_of(a_in, py * 4 + px)
                gs.append(ref[at, :, cols])
                ref, at = block_of(b_in, px * 4 + py)
                gs.append(ref[at, :CUBE, cols])
                stats.append(ref[at, CUBE:, cols])
            q = jnp.concatenate(qs, axis=0)
            g = jnp.concatenate(gs, axis=0)
            stat = jnp.concatenate(stats, axis=1).astype(F32)
            m = stat[0:1] + stat[1:2] + stat[2:3]
            total = stat[3:4] + stat[4:5] + stat[5:6]
            delta = stat[6:7] + stat[7:8] + stat[8:9]
            hit = []
            for c in range(2):
                own = cube0 + float(c)
                hit.append(
                    (stat[9:10] == own) | (stat[10:11] == own)
                    | (stat[11:12] == own) | (stat[12:13] == own)
                )
            bias = jnp.concatenate(
                [jnp.broadcast_to(jnp.where(z, 0.0, 1.0), (CUBE, z.shape[1])) for z in hit], axis=0
            )
            s = dot(k, q, NT) * scale
            p = jnp.exp(jnp.where(bias > 0.5, -1e30, s - m)) / total
            dv = dv + dot(p.astype(BF16), g)
            dp = dot(v, g, NT)
            ds = (scale * p * (dp - delta)).astype(BF16)
            dk = dk + dot(ds, q)
            pool = pool_matrix(32, 8 * CUBE, 8 * py)
            qsum = qsum + dot(pool, q)
            gsum = gsum + dot(pool, g)
        qc = (qsum * (1.0 / CUBE)).astype(BF16)
        gc = gsum.astype(BF16)
        kc, vc = kc_ref[:, cols], vc_ref[:, cols]
        cp, _, _ = softmax_parts(dot(kc, qc, NT) * scale, 0)
        cdv = dot(cp.astype(BF16), gc) * (1.0 / CUBE)
        cdp = dot(vc, gc, NT)
        cds = (scale * cp * (cdp - jnp.sum(cp * cdp, axis=0, keepdims=True))).astype(BF16)
        cdk = dot(cds, qc) * (1.0 / CUBE)
        for c in range(2):
            toks = slice(c * CUBE, c * CUBE + CUBE)
            dk_ref[toks, cols] = (dk[toks] + cdk[c : c + 1]).astype(BF16)
            dv_ref[toks, cols] = (dv[toks] + cdv[c : c + 1]).astype(BF16)


def join_kernel(meta, *rest):
    a_in, b_in = rest[:5], rest[5:10]
    out_ref = rest[10]
    half = a_in[0].shape[2]
    y, x = meta[8], meta[9]
    for py in range(4):
        for px in range(4):
            dev = lax.rem(y + OFFS[py] + SIDE, SIDE) * SIDE + lax.rem(x + OFFS[px] + SIDE, SIDE)
            ref, at = block_of(a_in, py * 4 + px)
            out_ref[dev, :, :half] = ref[at]
            ref, at = block_of(b_in, px * 4 + py)
            out_ref[dev, :, half:] = ref[at]


def vmem_call(body, outs, args, scratch=(), limit=40 << 20):
    smem = pl.BlockSpec(memory_space=pltpu.SMEM)
    vmem = pl.BlockSpec(memory_space=pltpu.VMEM)
    return pl.pallas_call(
        body,
        out_shape=[jax.ShapeDtypeStruct(shape, dtype) for shape, dtype in outs],
        in_specs=[smem] + [vmem] * (len(args) - 1),
        out_specs=[vmem] * len(outs),
        scratch_shapes=list(scratch),
        compiler_params=pltpu.CompilerParams(vmem_limit_bytes=limit),
    )(*args)


def on_device(queries, key_states, value_states, layer_grad, out_weight, chosen):
    scale = HD ** (-0.5)
    query, key, value, layer = queries[0], key_states[0], value_states[0], layer_grad[0]
    tokens, width = query.shape
    clips = 4
    cut = layer.shape[1] // clips
    ctx = lax.axis_index("ctx")
    clip = lax.axis_index("clip")
    meta = jnp.concatenate(
        [chosen.reshape(-1), jnp.stack([ctx // SIDE, ctx % SIDE]).astype(jnp.int32)]
    )

    def to_clip(v, by):
        return lax.ppermute(v, "clip", [(i, (i + by) % clips) for i in range(clips)])

    cols = []
    for d in range(clips):
        mine = lax.dynamic_slice_in_dim(layer, lax.rem(clip + d, clips) * cut, cut, axis=1)
        cols.append(to_clip(mine, d) if d else mine)
    columns = jnp.concatenate(cols, axis=0)
    keys = spread(key, "x")
    values = spread(value, "y")
    partial = dot(columns, out_weight, NT)
    grads = [partial[:tokens]]
    for d in range(1, clips):
        grads.append(to_clip(partial[d * tokens : (d + 1) * tokens].astype(BF16), -d))
    query_all = lax.all_gather(query, "ctx", axis=0)
    att, dq, da, db, kc, vc = vmem_call(
        functools.partial(query_kernel, scale),
        [
            ((tokens, width), BF16),
            ((tokens, width), BF16),
            ((CUBE, width), BF16),
            ((CUBE + STAT, width), BF16),
            ((32, width), BF16),
            ((32, width), BF16),
        ],
        [meta, query, *grads, *keys, *values],
        scratch=[
            pltpu.VMEM((32, CUBE, width), BF16),
            pltpu.VMEM((32, CUBE, width), BF16),
            pltpu.VMEM((tokens, width), BF16),
        ],
    )
    atts = jnp.concatenate([att] + [to_clip(att, d) for d in range(1, clips)], axis=0)
    term = lax.dot_general(atts, columns, (((0,), (0,)), ((), ())), preferred_element_type=F32)
    term = term.astype(BF16).reshape(SIDE * SIDE, -1, cut)
    terms = lax.all_to_all(term, "ctx", 0, 0, tiled=True)
    total = jnp.sum(terms.astype(F32), axis=0).astype(BF16)
    das = spread(da, "x")
    dbs = spread(db, "y")
    dk, dv = vmem_call(
        functools.partial(key_kernel, scale),
        [((tokens, width), BF16), ((tokens, width), BF16)],
        [meta, query_all, key, value, kc, vc, *das, *dbs],
    )
    half = cut // 2
    (weight,) = vmem_call(
        join_kernel,
        [(term.shape, BF16)],
        [meta, *spread(total[:, :half], "x"), *spread(total[:, half:], "y")],
    )
    return att[None], dq[None], dk[None], dv[None], weight.reshape(width, cut)


def solution(mesh):
    assert mesh.shape["ctx"] == SIDE * SIDE and mesh.shape["clip"] == 4
    tokens = P("clip", "ctx", "head")
    layer = P("clip", "ctx", None)
    weight = P("head", "clip")
    return jax.shard_map(
        on_device,
        mesh=mesh,
        in_specs=(tokens, tokens, tokens, layer, weight, layer),
        out_specs=(tokens, tokens, tokens, tokens, weight),
        check_vma=False,
    )
```

```python
import functools

import jax
import jax.numpy as jnp
from jax import lax
from jax.experimental import pallas as pl
from jax.experimental.pallas import tpu as pltpu
from jax.sharding import PartitionSpec as P

HD = 128
CUBE = 64
SIDE = 4
OFFS = (0, -1, 1, 2)
STAT = 16
F32 = jnp.float32
BF16 = jnp.bfloat16
NT = (((1,), (1,)), ((), ()))
NN = (((1,), (0,)), ((), ()))


def dot(a, b, dims=NN):
    return lax.dot_general(a, b, dims, preferred_element_type=F32)


def shift(v, along, by):
    pairs = []
    for y in range(SIDE):
        for x in range(SIDE):
            to = y * SIDE + (x + by) % SIDE if along == "x" else (y + by) % SIDE * SIDE + x
            pairs.append((y * SIDE + x, to))
    return lax.ppermute(v, "ctx", pairs)


def ends(v, along):
    return shift(v, along, 1), shift(v, along, -1)


def far(low, high, along):
    cut = low.shape[0] // 2 // 8 * 8
    return shift(low[:cut], along, 1), shift(high[cut:], along, -1)


def row_of(v, along):
    low, high = ends(v, along)
    return jnp.concatenate([v, low, high, *far(low, high, along)])


def blocks_of(parts, n):
    return [part.reshape(-1, n, part.shape[1]) for part in parts]


def after(v, *others):
    return lax.optimization_barrier((v, *others))[0]


def pool_matrix(rows, tokens, base):
    r = lax.broadcasted_iota(jnp.int32, (rows, tokens), 0)
    t = lax.broadcasted_iota(jnp.int32, (rows, tokens), 1)
    lo = (r - base) * CUBE
    return jnp.where((t >= lo) & (t < lo + CUBE), 1.0, 0.0).astype(BF16)


def place_of(delta):
    d = jnp.where(delta < 0, delta + SIDE, delta)
    return jnp.where(d < 2, 2 * d, 7 - 2 * d)


def softmax_parts(s, axis):
    m = jnp.max(s, axis=axis, keepdims=True)
    e = jnp.exp(s - m)
    total = jnp.sum(e, axis=axis, keepdims=True)
    return e / total, m, total


def pieces_of(v):
    a = v.astype(BF16)
    rest = v - a.astype(F32)
    b = rest.astype(BF16)
    return a, b, (rest - b.astype(F32)).astype(BF16)


def load_blocks(parts, dst, sem):
    copies, at = [], 0
    for part in parts:
        n = part.shape[0]
        copies.append(pltpu.make_async_copy(part, dst.at[pl.ds(at, n)], sem.at[len(copies)]))
        at += n
    for copy in copies:
        copy.start()
    return copies


def query_kernel(scale, meta, q_ref, dall, *rest):
    k_in, v_in = rest[:5], rest[5:10]
    att_ref, rel_ref, dq_ref, stat_ref, kc_ref, vc_ref, kall, vall, ksem, vsem = rest[10:]
    heads = q_ref.shape[1] // HD
    tokens = q_ref.shape[0]
    copies = load_blocks(k_in, kall, ksem) + load_blocks(v_in, vall, vsem)
    core = meta[10]
    grad = dall[...]
    for copy in copies:
        copy.wait()
    pool8 = pool_matrix(8, 8 * CUBE, 0)
    i0 = lax.broadcasted_iota(jnp.int32, (32, 32), 0)
    i1 = lax.broadcasted_iota(jnp.int32, (32, 32), 1)
    y, x = meta[8], meta[9]
    partner = ((i0 // 2) % 4) * 8 + (i0 // 8) * 2 + i0 % 2
    swap = jnp.where(i1 == partner, 1.0, 0.0).astype(BF16)

    def means(src):
        rows = [
            dot(pool8, src[4 * p : 4 * p + 4].reshape(8 * CUBE, heads * HD)) for p in range(4)
        ]
        return (jnp.concatenate(rows, axis=0) * (1.0 / CUBE)).astype(BF16)

    kc = means(kall)
    vc = dot(swap, means(vall)).astype(BF16)
    kc_ref[...] = kc
    vc_ref[...] = vc
    pool2 = pool_matrix(8, tokens, 0)
    qc = (dot(pool2, q_ref[...]) * (1.0 / CUBE)).astype(BF16)
    gc = dot(pool2, grad).astype(BF16)
    eye = lax.broadcasted_iota(jnp.int32, (CUBE, HD), 0)
    lane = lax.broadcasted_iota(jnp.int32, (CUBE, HD), 1)
    kslot, vslot = [], []
    for c in range(2):
        for j in range(4):
            cube = meta[4 * c + j]
            dev = cube // 2
            py = place_of(dev // SIDE - y)
            px = place_of(dev % SIDE - x)
            kslot.append((py * 4 + px, pl.multiple_of(cube % 2 * CUBE, CUBE)))
            vslot.append((px * 4 + py, pl.multiple_of(cube % 2 * CUBE, CUBE)))
    parts = [slice(h * HD, h * HD + HD) for h in range(heads)]
    cs = [dot(qc[:, cols], kc[:, cols], NT) * scale for cols in parts]
    cdp = [dot(gc[:, cols], vc[:, cols], NT) for cols in parts]
    cp = [softmax_parts(z, 1)[0] for z in cs]
    cout = [dot(z.astype(BF16), vc[:, cols]) for z, cols in zip(cp, parts)]
    cds = [
        (scale * z * (w - jnp.sum(z * w, axis=1, keepdims=True))).astype(BF16)
        for z, w in zip(cp, cdp)
    ]
    cdq = [dot(z, kc[:, cols]) * (1.0 / CUBE) for z, cols in zip(cds, parts)]

    def picked(ref, slots, cols):
        return jnp.concatenate([ref[at, pl.ds(low, CUBE), cols] for at, low in slots], axis=0)

    def put(row, h, value):
        low = (row // 8 * heads + h) * HD
        stat_ref[row % 8 : row % 8 + 1, low : low + HD] = value

    stat_ref[...] = jnp.zeros_like(stat_ref)
    stats = []
    for c in range(2):
        toks = slice(c * CUBE, c * CUBE + CUBE)
        turn = core if c == 0 else 1 - core
        ks, vs = kslot[4 * c : 4 * c + 4], vslot[4 * c : 4 * c + 4]
        scores = [dot(q_ref[toks, cols], picked(kall, ks, cols), NT) * scale for cols in parts]
        dps = [dot(dall[toks, cols], picked(vall, vs, cols), NT) for cols in parts]
        soft = [softmax_parts(z, 1) for z in scores]
        for h, cols in enumerate(parts):
            out = dot(soft[h][0].astype(BF16), picked(vall, vs, cols)) + cout[h][c : c + 1]
            att_ref[toks, cols] = out.astype(BF16)
            rel_ref[turn, :, cols] = out.astype(BF16)
        deltas = [jnp.sum(z[0] * w, axis=1, keepdims=True) for z, w in zip(soft, dps)]
        ds = [(scale * z[0] * (w - d)).astype(BF16) for z, w, d in zip(soft, dps, deltas)]
        for h, cols in enumerate(parts):
            dq = dot(ds[h], picked(kall, ks, cols)) + cdq[h][c : c + 1]
            dq_ref[toks, cols] = dq.astype(BF16)
        stats.append([(z[1], z[2], d) for z, d in zip(soft, deltas)])
    for h, cols in enumerate(parts):
        for n in range(3):
            row = jnp.zeros((1, HD), F32)
            for c in range(2):
                on = lane == eye + c * CUBE
                row = row + jnp.sum(jnp.where(on, stats[c][h][n], 0.0), axis=0, keepdims=True)
            for e, piece in enumerate(pieces_of(row)):
                put(3 * n + e, h, piece)
    lane1 = lax.broadcasted_iota(jnp.int32, (1, HD), 1)
    for j in range(4):
        pick = jnp.where(lane1 < CUBE, meta[j], meta[4 + j]).astype(F32).astype(BF16)
        for h in range(heads):
            put(9 + j, h, pick)


def key_kernel(scale, meta, stat_ref, k_ref, v_ref, kc_ref, vc_ref, *rest):
    dk_ref, dv_ref, q_all, g_all, qsem, gsem = rest[10:]
    copies = load_blocks(rest[:5], q_all, qsem) + load_blocks(rest[5:10], g_all, gsem)
    for copy in copies:
        copy.wait()
    heads = k_ref.shape[1] // HD
    y, x = meta[8], meta[9]
    cube0 = (2 * (y * SIDE + x)).astype(F32)
    for h in range(heads):
        cols = slice(h * HD, h * HD + HD)
        k, v = k_ref[:, cols], v_ref[:, cols]

        def gathered(side):
            qs, gs, stats = [], [], []
            for px in range(4):
                dev = lax.rem(y + OFFS[side] + SIDE, SIDE) * SIDE + lax.rem(x + OFFS[px] + SIDE, SIDE)
                qs.append(q_all[side * 4 + px, :, cols])
                gs.append(g_all[px * 4 + side, :, cols])
                at = [slice((n * heads + h) * HD, (n * heads + h) * HD + HD) for n in range(2)]
                stats.append(jnp.concatenate([stat_ref[dev, :, z] for z in at], axis=0))
            stat = jnp.concatenate(stats, axis=1).astype(F32)
            sums = [stat[n : n + 1] + stat[n + 1 : n + 2] + stat[n + 2 : n + 3] for n in (0, 3, 6)]
            return jnp.concatenate(qs, axis=0), jnp.concatenate(gs, axis=0), sums, stat[9:13]

        def bias(picks):
            rows = []
            for c in range(2):
                away = jnp.min(jnp.abs(picks - (cube0 + float(c))), axis=0, keepdims=True)
                rows.append(jnp.broadcast_to(away, (CUBE, away.shape[1])))
            return jnp.concatenate(rows, axis=0)

        sides = [gathered(side) for side in range(4)]
        scores = [dot(k, z[0], NT) * scale for z in sides]
        dps = [dot(v, z[1], NT) for z in sides]
        ps = [
            jnp.exp(jnp.where(bias(z[3]) > 0.5, -1e30, s - z[2][0])) / z[2][1]
            for s, z in zip(scores, sides)
        ]
        dv = sum(dot(p.astype(BF16), z[1]) for p, z in zip(ps, sides))
        ds = [(scale * p * (w - z[2][2])).astype(BF16) for p, w, z in zip(ps, dps, sides)]
        dk = sum(dot(w, z[0]) for w, z in zip(ds, sides))
        pools = [pool_matrix(32, 8 * CUBE, 8 * side) for side in range(4)]
        qc = (sum(dot(w, z[0]) for w, z in zip(pools, sides)) * (1.0 / CUBE)).astype(BF16)
        gc = sum(dot(w, z[1]) for w, z in zip(pools, sides)).astype(BF16)
        kc, vc = kc_ref[:, cols], vc_ref[:, cols]
        cp, _, _ = softmax_parts(dot(kc, qc, NT) * scale, 0)
        cdv = dot(cp.astype(BF16), gc) * (1.0 / CUBE)
        cdp = dot(vc, gc, NT)
        cds = (scale * cp * (cdp - jnp.sum(cp * cdp, axis=0, keepdims=True))).astype(BF16)
        cdk = dot(cds, qc) * (1.0 / CUBE)
        for c in range(2):
            toks = slice(c * CUBE, c * CUBE + CUBE)
            dk_ref[toks, cols] = (dk[toks] + cdk[c : c + 1]).astype(BF16)
            dv_ref[toks, cols] = (dv[toks] + cdv[c : c + 1]).astype(BF16)


def local_call(body, outs, args, left, scratch, cost):
    smem = pl.BlockSpec(memory_space=pltpu.SMEM)
    vmem = pl.BlockSpec(memory_space=pltpu.VMEM)
    stay = pl.BlockSpec(memory_space=pl.ANY)
    specs = [smem] + [stay if left(n) else vmem for n in range(1, len(args))]
    return pl.pallas_call(
        body,
        out_shape=[jax.ShapeDtypeStruct(shape, BF16) for shape in outs],
        in_specs=specs,
        out_specs=[vmem] * len(outs),
        scratch_shapes=list(scratch),
        compiler_params=pltpu.CompilerParams(vmem_limit_bytes=32 << 20),
        cost_estimate=cost,
    )(*args)


def on_device(queries, key_states, value_states, layer_grad, out_weight, chosen):
    scale = HD ** (-0.5)
    query, key, value, layer = queries[0], key_states[0], value_states[0], layer_grad[0]
    tokens, width = query.shape
    clips = 4
    cut = layer.shape[1] // clips
    ctx = lax.axis_index("ctx")
    clip = lax.axis_index("clip")
    core = lax.axis_index("head") % 2
    meta = jnp.concatenate(
        [chosen.reshape(-1), jnp.stack([ctx // SIDE, ctx % SIDE, core]).astype(jnp.int32)]
    )

    def to_clip(v, by):
        return lax.ppermute(v, "clip", [(i, (i + by) % clips) for i in range(clips)])

    halves = []
    for d in range(1, clips):
        start = (core * CUBE, lax.rem(clip + d, clips) * cut)
        halves.append(to_clip(lax.dynamic_slice(layer, start, (CUBE, cut)), d))
    key_row, value_row = row_of(key, "x"), row_of(value, "y")
    keys = [key_row, *ends(key_row, "y")]
    values = [value_row, *ends(value_row, "x")]
    near = (*keys[1:], *values[1:])
    keys += far(*near[:2], "y")
    values += far(*near[2:], "x")
    own = lax.dynamic_slice_in_dim(layer, clip * cut, cut, axis=1)
    halves = jnp.stack(lax.optimization_barrier((*halves, key_row, value_row))[: clips - 1])
    there = lax.ppermute(halves, "head", [(h, h ^ 1) for h in range(4)])
    others = jnp.stack([halves, there], axis=1).reshape(-1, cut)
    first = dot(own, out_weight, NT)
    partial = dot(others, out_weight, NT).astype(BF16).reshape(clips - 1, 2, CUBE, width)
    grads = [to_clip(partial[d - 1], -d) for d in range(1, clips)]
    grad = sum(z.astype(F32) for z in grads)
    swap = core * CUBE
    grad = lax.dynamic_slice_in_dim(
        jnp.concatenate([grad[0], grad[1], grad[0]]), swap, tokens, axis=0
    )
    grad = (first + grad).astype(BF16)
    query_row = row_of(after(query, *near), "x")
    blocks = SIDE * SIDE
    att, rel, dq, stat, kc, vc = local_call(
        functools.partial(query_kernel, scale),
        [
            (tokens, width),
            (2, CUBE, width),
            (tokens, width),
            (STAT // 2, 2 * width),
            (32, width),
            (32, width),
        ],
        [meta, query, grad, *blocks_of(keys, tokens), *blocks_of(values, tokens)],
        lambda n: n >= 3,
        [
            pltpu.VMEM((blocks, tokens, width), BF16),
            pltpu.VMEM((blocks, tokens, width), BF16),
            pltpu.SemaphoreType.DMA((5,)),
            pltpu.SemaphoreType.DMA((5,)),
        ],
        pl.CostEstimate(flops=1 << 32, transcendentals=1 << 18, bytes_accessed=6 << 20),
    )
    grad_row = row_of(after(grad, stat), "y")
    away = [to_clip(rel, d).reshape(tokens, width) for d in range(1, clips)]
    *away, grad_row, query_row = lax.optimization_barrier((*away, grad_row, query_row))
    atts = jnp.concatenate([att, *away], axis=0)
    columns = jnp.concatenate([own, others], axis=0)
    term = lax.dot_general(atts, columns, (((0,), (0,)), ((), ())), preferred_element_type=F32)
    term = term.astype(BF16).reshape(blocks, -1, cut)
    queries_all = [query_row, *ends(query_row, "y")]
    grads_all = [grad_row, *ends(grad_row, "x")]
    term = after(term, *queries_all[1:], *grads_all[1:])
    stats = jnp.broadcast_to(stat[None], (blocks, *stat.shape))
    terms = lax.all_to_all(jnp.concatenate([term, stats], axis=1), "ctx", 0, 0, tiled=True)
    queries_all += far(*queries_all[1:], "y")
    grads_all += far(*grads_all[1:], "x")
    terms = after(terms, *queries_all[3:], *grads_all[3:])
    rows = term.shape[1]
    total = jnp.sum(terms[:, :rows].astype(F32), axis=0).astype(BF16)
    dk, dv = local_call(
        functools.partial(key_kernel, scale),
        [(tokens, width), (tokens, width)],
        [
            meta,
            terms[:, rows:],
            after(key, total),
            value,
            kc,
            vc,
            *blocks_of(queries_all, tokens),
            *blocks_of(grads_all, tokens),
        ],
        lambda n: n >= 6,
        [
            pltpu.VMEM((blocks, tokens, width), BF16),
            pltpu.VMEM((blocks, tokens, width), BF16),
            pltpu.SemaphoreType.DMA((5,)),
            pltpu.SemaphoreType.DMA((5,)),
        ],
        pl.CostEstimate(flops=1 << 33, transcendentals=1 << 21, bytes_accessed=6 << 20),
    )
    copies = jnp.broadcast_to(total[None], (blocks, *total.shape))
    weight = lax.all_to_all(copies, "ctx", 0, 0, tiled=True)
    weight, dk, dv = lax.optimization_barrier((weight, dk, dv))
    return att[None], dq[None], dk[None], dv[None], weight.reshape(width, cut)


def solution(mesh):
    assert mesh.shape["ctx"] == SIDE * SIDE and mesh.shape["clip"] == 4
    tokens = P("clip", "ctx", "head")
    layer = P("clip", "ctx", None)
    weight = P("head", "clip")
    return jax.shard_map(
        on_device,
        mesh=mesh,
        in_specs=(tokens, tokens, tokens, layer, weight, layer),
        out_specs=(tokens, tokens, tokens, tokens, weight),
        check_vma=False,
    )
```

```python
import functools

import jax
import jax.numpy as jnp
from jax import lax
from jax.experimental import pallas as pl
from jax.experimental.pallas import tpu as pltpu
from jax.sharding import PartitionSpec as P

HD = 128
CUBE = 64
SIDE = 4
OFFS = (0, -1, 1, 2)
STAT = 16
F32 = jnp.float32
BF16 = jnp.bfloat16
NT = (((1,), (1,)), ((), ()))
NN = (((1,), (0,)), ((), ()))


def dot(a, b, dims=NN):
    return lax.dot_general(a, b, dims, preferred_element_type=F32)


def shift(v, along, by):
    pairs = []
    for y in range(SIDE):
        for x in range(SIDE):
            to = y * SIDE + (x + by) % SIDE if along == "x" else (y + by) % SIDE * SIDE + x
            pairs.append((y * SIDE + x, to))
    return lax.ppermute(v, "ctx", pairs)


def ends(v, along):
    return shift(v, along, 1), shift(v, along, -1)


def far(low, high, along):
    cut = low.shape[0] // 2 // 8 * 8
    return shift(low[:cut], along, 1), shift(high[cut:], along, -1)


def join_kernel(*refs):
    out, at = refs[-1], 0
    for ref in refs[:-1]:
        out[at : at + ref.shape[0]] = ref[...]
        at += ref.shape[0]


def join(parts):
    vmem = pl.BlockSpec(memory_space=pltpu.VMEM)
    rows = sum(part.shape[0] for part in parts)
    return pl.pallas_call(
        join_kernel,
        out_shape=jax.ShapeDtypeStruct((rows, parts[0].shape[1]), BF16),
        in_specs=[vmem] * len(parts),
        out_specs=vmem,
        compiler_params=pltpu.CompilerParams(vmem_limit_bytes=8 << 20),
        cost_estimate=pl.CostEstimate(flops=1 << 20, transcendentals=0, bytes_accessed=1 << 20),
    )(*parts)


def row_of(v, along):
    low, high = ends(v, along)
    return join([v, low, high, *far(low, high, along)])


def blocks_of(parts, n):
    return [part.reshape(-1, n, part.shape[1]) for part in parts]


def after(v, *others):
    return lax.optimization_barrier((v, *others))[0]


def pool_matrix(rows, tokens, base):
    r = lax.broadcasted_iota(jnp.int32, (rows, tokens), 0)
    t = lax.broadcasted_iota(jnp.int32, (rows, tokens), 1)
    lo = (r - base) * CUBE
    return jnp.where((t >= lo) & (t < lo + CUBE), 1.0, 0.0).astype(BF16)


def place_of(delta):
    d = jnp.where(delta < 0, delta + SIDE, delta)
    return jnp.where(d < 2, 2 * d, 7 - 2 * d)


def softmax_parts(s, axis):
    m = jnp.max(s, axis=axis, keepdims=True)
    e = jnp.exp(s - m)
    total = jnp.sum(e, axis=axis, keepdims=True)
    return e / total, m, total


def pieces_of(v):
    a = v.astype(BF16)
    rest = v - a.astype(F32)
    b = rest.astype(BF16)
    return a, b, (rest - b.astype(F32)).astype(BF16)


def load_blocks(parts, dst, sem):
    copies, at = [], 0
    for part in parts:
        n = part.shape[0]
        copies.append(pltpu.make_async_copy(part, dst.at[pl.ds(at, n)], sem.at[len(copies)]))
        at += n
    for copy in copies:
        copy.start()
    return copies


def query_kernel(scale, meta, q_ref, dall, *rest):
    k_in, v_in = rest[:5], rest[5:10]
    att_ref, rel_ref, dq_ref, stat_ref, kc_ref, vc_ref, kall, vall, ksem, vsem = rest[10:]
    heads = q_ref.shape[1] // HD
    tokens = q_ref.shape[0]
    copies = load_blocks(k_in, kall, ksem) + load_blocks(v_in, vall, vsem)
    core = meta[10]
    grad = dall[...]
    for copy in copies:
        copy.wait()
    pool8 = pool_matrix(8, 8 * CUBE, 0)
    i0 = lax.broadcasted_iota(jnp.int32, (32, 32), 0)
    i1 = lax.broadcasted_iota(jnp.int32, (32, 32), 1)
    y, x = meta[8], meta[9]
    partner = ((i0 // 2) % 4) * 8 + (i0 // 8) * 2 + i0 % 2
    swap = jnp.where(i1 == partner, 1.0, 0.0).astype(BF16)

    def means(src):
        rows = [
            dot(pool8, src[4 * p : 4 * p + 4].reshape(8 * CUBE, heads * HD)) for p in range(4)
        ]
        return (jnp.concatenate(rows, axis=0) * (1.0 / CUBE)).astype(BF16)

    kc = means(kall)
    vc = dot(swap, means(vall)).astype(BF16)
    kc_ref[...] = kc
    vc_ref[...] = vc
    pool2 = pool_matrix(8, tokens, 0)
    qc = (dot(pool2, q_ref[...]) * (1.0 / CUBE)).astype(BF16)
    gc = dot(pool2, grad).astype(BF16)
    eye = lax.broadcasted_iota(jnp.int32, (CUBE, HD), 0)
    lane = lax.broadcasted_iota(jnp.int32, (CUBE, HD), 1)
    kslot, vslot = [], []
    for c in range(2):
        for j in range(4):
            cube = meta[4 * c + j]
            dev = cube // 2
            py = place_of(dev // SIDE - y)
            px = place_of(dev % SIDE - x)
            kslot.append((py * 4 + px, pl.multiple_of(cube % 2 * CUBE, CUBE)))
            vslot.append((px * 4 + py, pl.multiple_of(cube % 2 * CUBE, CUBE)))
    parts = [slice(h * HD, h * HD + HD) for h in range(heads)]
    cs = [dot(qc[:, cols], kc[:, cols], NT) * scale for cols in parts]
    cdp = [dot(gc[:, cols], vc[:, cols], NT) for cols in parts]
    cp = [softmax_parts(z, 1)[0] for z in cs]
    cout = [dot(z.astype(BF16), vc[:, cols]) for z, cols in zip(cp, parts)]
    cds = [
        (scale * z * (w - jnp.sum(z * w, axis=1, keepdims=True))).astype(BF16)
        for z, w in zip(cp, cdp)
    ]
    cdq = [dot(z, kc[:, cols]) * (1.0 / CUBE) for z, cols in zip(cds, parts)]

    def picked(ref, slots, cols):
        return jnp.concatenate([ref[at, pl.ds(low, CUBE), cols] for at, low in slots], axis=0)

    def put(row, h, value):
        low = (row // 8 * heads + h) * HD
        stat_ref[row % 8 : row % 8 + 1, low : low + HD] = value

    stat_ref[...] = jnp.zeros_like(stat_ref)
    stats = []
    for c in range(2):
        toks = slice(c * CUBE, c * CUBE + CUBE)
        turn = core if c == 0 else 1 - core
        ks, vs = kslot[4 * c : 4 * c + 4], vslot[4 * c : 4 * c + 4]
        scores = [dot(q_ref[toks, cols], picked(kall, ks, cols), NT) * scale for cols in parts]
        dps = [dot(dall[toks, cols], picked(vall, vs, cols), NT) for cols in parts]
        soft = [softmax_parts(z, 1) for z in scores]
        for h, cols in enumerate(parts):
            out = dot(soft[h][0].astype(BF16), picked(vall, vs, cols)) + cout[h][c : c + 1]
            att_ref[toks, cols] = out.astype(BF16)
            rel_ref[turn, :, cols] = out.astype(BF16)
        deltas = [jnp.sum(z[0] * w, axis=1, keepdims=True) for z, w in zip(soft, dps)]
        ds = [(scale * z[0] * (w - d)).astype(BF16) for z, w, d in zip(soft, dps, deltas)]
        for h, cols in enumerate(parts):
            dq = dot(ds[h], picked(kall, ks, cols)) + cdq[h][c : c + 1]
            dq_ref[toks, cols] = dq.astype(BF16)
        stats.append([(z[1], z[2], d) for z, d in zip(soft, deltas)])
    for h, cols in enumerate(parts):
        for n in range(3):
            row = jnp.zeros((1, HD), F32)
            for c in range(2):
                on = lane == eye + c * CUBE
                row = row + jnp.sum(jnp.where(on, stats[c][h][n], 0.0), axis=0, keepdims=True)
            for e, piece in enumerate(pieces_of(row)):
                put(3 * n + e, h, piece)
    lane1 = lax.broadcasted_iota(jnp.int32, (1, HD), 1)
    for j in range(4):
        pick = jnp.where(lane1 < CUBE, meta[j], meta[4 + j]).astype(F32).astype(BF16)
        for h in range(heads):
            put(9 + j, h, pick)


def key_kernel(scale, meta, stat_ref, k_ref, v_ref, kc_ref, vc_ref, *rest):
    dk_ref, dv_ref, q_all, g_all, qsem, gsem = rest[10:]
    copies = load_blocks(rest[:5], q_all, qsem) + load_blocks(rest[5:10], g_all, gsem)
    for copy in copies:
        copy.wait()
    heads = k_ref.shape[1] // HD
    y, x = meta[8], meta[9]
    cube0 = (2 * (y * SIDE + x)).astype(F32)
    for h in range(heads):
        cols = slice(h * HD, h * HD + HD)
        k, v = k_ref[:, cols], v_ref[:, cols]

        def gathered(side):
            qs, gs, stats = [], [], []
            for px in range(4):
                dev = lax.rem(y + OFFS[side] + SIDE, SIDE) * SIDE + lax.rem(x + OFFS[px] + SIDE, SIDE)
                qs.append(q_all[side * 4 + px, :, cols])
                gs.append(g_all[px * 4 + side, :, cols])
                at = [slice((n * heads + h) * HD, (n * heads + h) * HD + HD) for n in range(2)]
                stats.append(jnp.concatenate([stat_ref[dev, :, z] for z in at], axis=0))
            stat = jnp.concatenate(stats, axis=1).astype(F32)
            sums = [stat[n : n + 1] + stat[n + 1 : n + 2] + stat[n + 2 : n + 3] for n in (0, 3, 6)]
            return jnp.concatenate(qs, axis=0), jnp.concatenate(gs, axis=0), sums, stat[9:13]

        def bias(picks):
            rows = []
            for c in range(2):
                away = jnp.min(jnp.abs(picks - (cube0 + float(c))), axis=0, keepdims=True)
                rows.append(jnp.broadcast_to(away, (CUBE, away.shape[1])))
            return jnp.concatenate(rows, axis=0)

        sides = [gathered(side) for side in range(4)]
        scores = [dot(k, z[0], NT) * scale for z in sides]
        dps = [dot(v, z[1], NT) for z in sides]
        ps = [
            jnp.exp(jnp.where(bias(z[3]) > 0.5, -1e30, s - z[2][0])) / z[2][1]
            for s, z in zip(scores, sides)
        ]
        dv = sum(dot(p.astype(BF16), z[1]) for p, z in zip(ps, sides))
        ds = [(scale * p * (w - z[2][2])).astype(BF16) for p, w, z in zip(ps, dps, sides)]
        dk = sum(dot(w, z[0]) for w, z in zip(ds, sides))
        pools = [pool_matrix(32, 8 * CUBE, 8 * side) for side in range(4)]
        qc = (sum(dot(w, z[0]) for w, z in zip(pools, sides)) * (1.0 / CUBE)).astype(BF16)
        gc = sum(dot(w, z[1]) for w, z in zip(pools, sides)).astype(BF16)
        kc, vc = kc_ref[:, cols], vc_ref[:, cols]
        cp, _, _ = softmax_parts(dot(kc, qc, NT) * scale, 0)
        cdv = dot(cp.astype(BF16), gc) * (1.0 / CUBE)
        cdp = dot(vc, gc, NT)
        cds = (scale * cp * (cdp - jnp.sum(cp * cdp, axis=0, keepdims=True))).astype(BF16)
        cdk = dot(cds, qc) * (1.0 / CUBE)
        for c in range(2):
            toks = slice(c * CUBE, c * CUBE + CUBE)
            dk_ref[toks, cols] = (dk[toks] + cdk[c : c + 1]).astype(BF16)
            dv_ref[toks, cols] = (dv[toks] + cdv[c : c + 1]).astype(BF16)


def local_call(body, outs, args, left, scratch, cost):
    smem = pl.BlockSpec(memory_space=pltpu.SMEM)
    vmem = pl.BlockSpec(memory_space=pltpu.VMEM)
    stay = pl.BlockSpec(memory_space=pl.ANY)
    specs = [smem] + [stay if left(n) else vmem for n in range(1, len(args))]
    return pl.pallas_call(
        body,
        out_shape=[jax.ShapeDtypeStruct(shape, BF16) for shape in outs],
        in_specs=specs,
        out_specs=[vmem] * len(outs),
        scratch_shapes=list(scratch),
        compiler_params=pltpu.CompilerParams(vmem_limit_bytes=32 << 20),
        cost_estimate=cost,
    )(*args)


def on_device(queries, key_states, value_states, layer_grad, out_weight, chosen):
    scale = HD ** (-0.5)
    query, key, value, layer = queries[0], key_states[0], value_states[0], layer_grad[0]
    tokens, width = query.shape
    clips = 4
    cut = layer.shape[1] // clips
    ctx = lax.axis_index("ctx")
    clip = lax.axis_index("clip")
    core = lax.axis_index("head") % 2
    meta = jnp.concatenate(
        [chosen.reshape(-1), jnp.stack([ctx // SIDE, ctx % SIDE, core]).astype(jnp.int32)]
    )

    def to_clip(v, by):
        return lax.ppermute(v, "clip", [(i, (i + by) % clips) for i in range(clips)])

    halves = []
    for d in range(1, clips):
        start = (core * CUBE, lax.rem(clip + d, clips) * cut)
        halves.append(to_clip(lax.dynamic_slice(layer, start, (CUBE, cut)), d))
    key_row, value_row = row_of(key, "x"), row_of(value, "y")
    keys = [key_row, *ends(key_row, "y")]
    values = [value_row, *ends(value_row, "x")]
    near = (*keys[1:], *values[1:])
    keys += far(*near[:2], "y")
    values += far(*near[2:], "x")
    own = lax.dynamic_slice_in_dim(layer, clip * cut, cut, axis=1)
    halves = jnp.stack(lax.optimization_barrier((*halves, key_row, value_row))[: clips - 1])
    there = lax.ppermute(halves, "head", [(h, h ^ 1) for h in range(4)])
    others = jnp.stack([halves, there], axis=1).reshape(-1, cut)
    first = dot(own, out_weight, NT)
    partial = dot(others, out_weight, NT).astype(BF16).reshape(clips - 1, 2, CUBE, width)
    grads = [to_clip(partial[d - 1], -d) for d in range(1, clips)]
    grads = lax.optimization_barrier((*grads, *keys[3:], *values[3:]))[: clips - 1]
    grad = sum(z.astype(F32) for z in grads)
    swap = core * CUBE
    grad = lax.dynamic_slice_in_dim(
        jnp.concatenate([grad[0], grad[1], grad[0]]), swap, tokens, axis=0
    )
    grad = (first + grad).astype(BF16)
    query_row = row_of(after(query, *near), "x")
    grad_ends = ends(grad, "y")
    blocks = SIDE * SIDE
    att, rel, dq, stat, kc, vc = local_call(
        functools.partial(query_kernel, scale),
        [
            (tokens, width),
            (2, CUBE, width),
            (tokens, width),
            (STAT // 2, 2 * width),
            (32, width),
            (32, width),
        ],
        [meta, after(query, query_row, *grad_ends), grad, *blocks_of(keys, tokens), *blocks_of(values, tokens)],
        lambda n: n >= 3,
        [
            pltpu.VMEM((blocks, tokens, width), BF16),
            pltpu.VMEM((blocks, tokens, width), BF16),
            pltpu.SemaphoreType.DMA((5,)),
            pltpu.SemaphoreType.DMA((5,)),
        ],
        pl.CostEstimate(flops=1 << 32, transcendentals=1 << 18, bytes_accessed=6 << 20),
    )
    grad_low, grad_high, _ = lax.optimization_barrier((*grad_ends, stat))
    grad_row = join([grad, grad_low, grad_high, *far(grad_low, grad_high, "y")])
    away = [to_clip(rel, d).reshape(tokens, width) for d in range(1, clips)]
    *away, grad_row, query_row = lax.optimization_barrier((*away, grad_row, query_row))
    atts = jnp.concatenate([att, *away], axis=0)
    columns = jnp.concatenate([own, others], axis=0)
    term = lax.dot_general(atts, columns, (((0,), (0,)), ((), ())), preferred_element_type=F32)
    term = term.astype(BF16).reshape(blocks, -1, cut)
    queries_all = [query_row, *ends(query_row, "y")]
    grads_all = [grad_row, *ends(grad_row, "x")]
    term = after(term, *queries_all[1:], *grads_all[1:])
    stats = jnp.broadcast_to(stat[None], (blocks, *stat.shape))
    terms = lax.all_to_all(jnp.concatenate([term, stats], axis=1), "ctx", 0, 0, tiled=True)
    queries_all += far(*queries_all[1:], "y")
    grads_all += far(*grads_all[1:], "x")
    terms = after(terms, *queries_all[3:], *grads_all[3:])
    rows = term.shape[1]
    total = jnp.sum(terms[:, :rows].astype(F32), axis=0).astype(BF16)
    dk, dv = local_call(
        functools.partial(key_kernel, scale),
        [(tokens, width), (tokens, width)],
        [
            meta,
            terms[:, rows:],
            after(key, total),
            value,
            kc,
            vc,
            *blocks_of(queries_all, tokens),
            *blocks_of(grads_all, tokens),
        ],
        lambda n: n >= 6,
        [
            pltpu.VMEM((blocks, tokens, width), BF16),
            pltpu.VMEM((blocks, tokens, width), BF16),
            pltpu.SemaphoreType.DMA((5,)),
            pltpu.SemaphoreType.DMA((5,)),
        ],
        pl.CostEstimate(flops=1 << 33, transcendentals=1 << 21, bytes_accessed=6 << 20),
    )
    copies = jnp.broadcast_to(total[None], (blocks, *total.shape))
    weight = lax.all_to_all(copies, "ctx", 0, 0, tiled=True)
    weight, dk, dv = lax.optimization_barrier((weight, dk, dv))
    return att[None], dq[None], dk[None], dv[None], weight.reshape(width, cut)


def solution(mesh):
    assert mesh.shape["ctx"] == SIDE * SIDE and mesh.shape["clip"] == 4
    tokens = P("clip", "ctx", "head")
    layer = P("clip", "ctx", None)
    weight = P("head", "clip")
    return jax.shard_map(
        on_device,
        mesh=mesh,
        in_specs=(tokens, tokens, tokens, layer, weight, layer),
        out_specs=(tokens, tokens, tokens, tokens, weight),
        check_vma=False,
    )
```

```python
import functools

import jax
import jax.numpy as jnp
from jax import lax
from jax.experimental import pallas as pl
from jax.experimental.pallas import tpu as pltpu
from jax.sharding import PartitionSpec as P

HD = 128
CUBE = 64
SIDE = 4
OFFS = (0, -1, 1, 2)
STAT = 16
F32 = jnp.float32
BF16 = jnp.bfloat16
NT = (((1,), (1,)), ((), ()))
NN = (((1,), (0,)), ((), ()))


def dot(a, b, dims=NN):
    return lax.dot_general(a, b, dims, preferred_element_type=F32)


def shift(v, along, by):
    pairs = []
    for y in range(SIDE):
        for x in range(SIDE):
            to = y * SIDE + (x + by) % SIDE if along == "x" else (y + by) % SIDE * SIDE + x
            pairs.append((y * SIDE + x, to))
    return lax.ppermute(v, "ctx", pairs)


def ends(v, along):
    return shift(v, along, 1), shift(v, along, -1)


def far(low, high, along):
    cut = low.shape[0] // 2 // 8 * 8
    return shift(low[:cut], along, 1), shift(high[cut:], along, -1)


def join_kernel(*refs):
    out, at = refs[-1], 0
    for ref in refs[:-1]:
        out[at : at + ref.shape[0]] = ref[...]
        at += ref.shape[0]


def join(parts):
    vmem = pl.BlockSpec(memory_space=pltpu.VMEM)
    rows = sum(part.shape[0] for part in parts)
    return pl.pallas_call(
        join_kernel,
        out_shape=jax.ShapeDtypeStruct((rows, parts[0].shape[1]), BF16),
        in_specs=[vmem] * len(parts),
        out_specs=vmem,
        compiler_params=pltpu.CompilerParams(vmem_limit_bytes=8 << 20),
        cost_estimate=pl.CostEstimate(flops=1 << 20, transcendentals=0, bytes_accessed=1 << 20),
    )(*parts)


def row_of(v, along):
    return join([v, *ends(v, along), shift(v, along, 2)])


def blocks_of(parts, n):
    return [part.reshape(-1, n, part.shape[1]) for part in parts]


def after(v, *others):
    return lax.optimization_barrier((v, *others))[0]


def pool_matrix(rows, tokens, base):
    r = lax.broadcasted_iota(jnp.int32, (rows, tokens), 0)
    t = lax.broadcasted_iota(jnp.int32, (rows, tokens), 1)
    lo = (r - base) * CUBE
    return jnp.where((t >= lo) & (t < lo + CUBE), 1.0, 0.0).astype(BF16)


def place_of(delta):
    d = jnp.where(delta < 0, delta + SIDE, delta)
    return jnp.where(d < 2, 2 * d, 7 - 2 * d)


def softmax_parts(s, axis):
    m = jnp.max(s, axis=axis, keepdims=True)
    e = jnp.exp(s - m)
    total = jnp.sum(e, axis=axis, keepdims=True)
    return e / total, m, total


def pieces_of(v):
    a = v.astype(BF16)
    rest = v - a.astype(F32)
    b = rest.astype(BF16)
    return a, b, (rest - b.astype(F32)).astype(BF16)


def load_blocks(parts, dst, sem):
    copies, at = [], 0
    for part in parts:
        n = part.shape[0]
        copies.append(pltpu.make_async_copy(part, dst.at[pl.ds(at, n)], sem.at[len(copies)]))
        at += n
    for copy in copies:
        copy.start()
    return copies


def query_kernel(scale, meta, q_ref, dall, *rest):
    k_in, v_in = rest[:5], rest[5:10]
    att_ref, rel_ref, dq_ref, stat_ref, kc_ref, vc_ref, kall, vall, ksem, vsem = rest[10:]
    heads = q_ref.shape[1] // HD
    tokens = q_ref.shape[0]
    copies = load_blocks(k_in, kall, ksem) + load_blocks(v_in, vall, vsem)
    core = meta[10]
    grad = dall[...]
    for copy in copies:
        copy.wait()
    pool8 = pool_matrix(8, 8 * CUBE, 0)
    i0 = lax.broadcasted_iota(jnp.int32, (32, 32), 0)
    i1 = lax.broadcasted_iota(jnp.int32, (32, 32), 1)
    y, x = meta[8], meta[9]
    partner = ((i0 // 2) % 4) * 8 + (i0 // 8) * 2 + i0 % 2
    swap = jnp.where(i1 == partner, 1.0, 0.0).astype(BF16)

    def means(src):
        rows = [
            dot(pool8, src[4 * p : 4 * p + 4].reshape(8 * CUBE, heads * HD)) for p in range(4)
        ]
        return (jnp.concatenate(rows, axis=0) * (1.0 / CUBE)).astype(BF16)

    kc = means(kall)
    vc = dot(swap, means(vall)).astype(BF16)
    kc_ref[...] = kc
    vc_ref[...] = vc
    pool2 = pool_matrix(8, tokens, 0)
    qc = (dot(pool2, q_ref[...]) * (1.0 / CUBE)).astype(BF16)
    gc = dot(pool2, grad).astype(BF16)
    eye = lax.broadcasted_iota(jnp.int32, (CUBE, HD), 0)
    lane = lax.broadcasted_iota(jnp.int32, (CUBE, HD), 1)
    kslot, vslot = [], []
    for c in range(2):
        for j in range(4):
            cube = meta[4 * c + j]
            dev = cube // 2
            py = place_of(dev // SIDE - y)
            px = place_of(dev % SIDE - x)
            kslot.append((py * 4 + px, pl.multiple_of(cube % 2 * CUBE, CUBE)))
            vslot.append((px * 4 + py, pl.multiple_of(cube % 2 * CUBE, CUBE)))
    parts = [slice(h * HD, h * HD + HD) for h in range(heads)]
    cs = [dot(qc[:, cols], kc[:, cols], NT) * scale for cols in parts]
    cdp = [dot(gc[:, cols], vc[:, cols], NT) for cols in parts]
    cp = [softmax_parts(z, 1)[0] for z in cs]
    cout = [dot(z.astype(BF16), vc[:, cols]) for z, cols in zip(cp, parts)]
    cds = [
        (scale * z * (w - jnp.sum(z * w, axis=1, keepdims=True))).astype(BF16)
        for z, w in zip(cp, cdp)
    ]
    cdq = [dot(z, kc[:, cols]) * (1.0 / CUBE) for z, cols in zip(cds, parts)]

    def picked(ref, slots, cols):
        return jnp.concatenate([ref[at, pl.ds(low, CUBE), cols] for at, low in slots], axis=0)

    def put(row, h, value):
        low = (row // 8 * heads + h) * HD
        stat_ref[row % 8 : row % 8 + 1, low : low + HD] = value

    stat_ref[...] = jnp.zeros_like(stat_ref)
    stats = []
    for c in range(2):
        toks = slice(c * CUBE, c * CUBE + CUBE)
        turn = core if c == 0 else 1 - core
        ks, vs = kslot[4 * c : 4 * c + 4], vslot[4 * c : 4 * c + 4]
        scores = [dot(q_ref[toks, cols], picked(kall, ks, cols), NT) * scale for cols in parts]
        dps = [dot(dall[toks, cols], picked(vall, vs, cols), NT) for cols in parts]
        soft = [softmax_parts(z, 1) for z in scores]
        for h, cols in enumerate(parts):
            out = dot(soft[h][0].astype(BF16), picked(vall, vs, cols)) + cout[h][c : c + 1]
            att_ref[toks, cols] = out.astype(BF16)
            rel_ref[turn, :, cols] = out.astype(BF16)
        deltas = [jnp.sum(z[0] * w, axis=1, keepdims=True) for z, w in zip(soft, dps)]
        ds = [(scale * z[0] * (w - d)).astype(BF16) for z, w, d in zip(soft, dps, deltas)]
        for h, cols in enumerate(parts):
            dq = dot(ds[h], picked(kall, ks, cols)) + cdq[h][c : c + 1]
            dq_ref[toks, cols] = dq.astype(BF16)
        stats.append([(z[1], z[2], d) for z, d in zip(soft, deltas)])
    for h, cols in enumerate(parts):
        for n in range(3):
            row = jnp.zeros((1, HD), F32)
            for c in range(2):
                on = lane == eye + c * CUBE
                row = row + jnp.sum(jnp.where(on, stats[c][h][n], 0.0), axis=0, keepdims=True)
            for e, piece in enumerate(pieces_of(row)):
                put(3 * n + e, h, piece)
    lane1 = lax.broadcasted_iota(jnp.int32, (1, HD), 1)
    for j in range(4):
        pick = jnp.where(lane1 < CUBE, meta[j], meta[4 + j]).astype(F32).astype(BF16)
        for h in range(heads):
            put(9 + j, h, pick)


def key_kernel(scale, meta, stat_ref, k_ref, v_ref, kc_ref, vc_ref, *rest):
    dk_ref, dv_ref, q_all, g_all, qsem, gsem = rest[10:]
    copies = load_blocks(rest[:5], q_all, qsem) + load_blocks(rest[5:10], g_all, gsem)
    for copy in copies:
        copy.wait()
    heads = k_ref.shape[1] // HD
    y, x = meta[8], meta[9]
    cube0 = (2 * (y * SIDE + x)).astype(F32)
    for h in range(heads):
        cols = slice(h * HD, h * HD + HD)
        k, v = k_ref[:, cols], v_ref[:, cols]

        def gathered(side):
            qs, gs, stats = [], [], []
            for px in range(4):
                dev = lax.rem(y + OFFS[side] + SIDE, SIDE) * SIDE + lax.rem(x + OFFS[px] + SIDE, SIDE)
                qs.append(q_all[side * 4 + px, :, cols])
                gs.append(g_all[px * 4 + side, :, cols])
                at = [slice((n * heads + h) * HD, (n * heads + h) * HD + HD) for n in range(2)]
                stats.append(jnp.concatenate([stat_ref[dev, :, z] for z in at], axis=0))
            stat = jnp.concatenate(stats, axis=1).astype(F32)
            sums = [stat[n : n + 1] + stat[n + 1 : n + 2] + stat[n + 2 : n + 3] for n in (0, 3, 6)]
            return jnp.concatenate(qs, axis=0), jnp.concatenate(gs, axis=0), sums, stat[9:13]

        def bias(picks):
            rows = []
            for c in range(2):
                away = jnp.min(jnp.abs(picks - (cube0 + float(c))), axis=0, keepdims=True)
                rows.append(jnp.broadcast_to(away, (CUBE, away.shape[1])))
            return jnp.concatenate(rows, axis=0)

        sides = [gathered(side) for side in range(4)]
        scores = [dot(k, z[0], NT) * scale for z in sides]
        dps = [dot(v, z[1], NT) for z in sides]
        ps = [
            jnp.exp(jnp.where(bias(z[3]) > 0.5, -1e30, s - z[2][0])) / z[2][1]
            for s, z in zip(scores, sides)
        ]
        dv = sum(dot(p.astype(BF16), z[1]) for p, z in zip(ps, sides))
        ds = [(scale * p * (w - z[2][2])).astype(BF16) for p, w, z in zip(ps, dps, sides)]
        dk = sum(dot(w, z[0]) for w, z in zip(ds, sides))
        pools = [pool_matrix(32, 8 * CUBE, 8 * side) for side in range(4)]
        qc = (sum(dot(w, z[0]) for w, z in zip(pools, sides)) * (1.0 / CUBE)).astype(BF16)
        gc = sum(dot(w, z[1]) for w, z in zip(pools, sides)).astype(BF16)
        kc, vc = kc_ref[:, cols], vc_ref[:, cols]
        cp, _, _ = softmax_parts(dot(kc, qc, NT) * scale, 0)
        cdv = dot(cp.astype(BF16), gc) * (1.0 / CUBE)
        cdp = dot(vc, gc, NT)
        cds = (scale * cp * (cdp - jnp.sum(cp * cdp, axis=0, keepdims=True))).astype(BF16)
        cdk = dot(cds, qc) * (1.0 / CUBE)
        for c in range(2):
            toks = slice(c * CUBE, c * CUBE + CUBE)
            dk_ref[toks, cols] = (dk[toks] + cdk[c : c + 1]).astype(BF16)
            dv_ref[toks, cols] = (dv[toks] + cdv[c : c + 1]).astype(BF16)


def local_call(body, outs, args, left, scratch, cost):
    smem = pl.BlockSpec(memory_space=pltpu.SMEM)
    vmem = pl.BlockSpec(memory_space=pltpu.VMEM)
    stay = pl.BlockSpec(memory_space=pl.ANY)
    specs = [smem] + [stay if left(n) else vmem for n in range(1, len(args))]
    return pl.pallas_call(
        body,
        out_shape=[jax.ShapeDtypeStruct(shape, BF16) for shape in outs],
        in_specs=specs,
        out_specs=[vmem] * len(outs),
        scratch_shapes=list(scratch),
        compiler_params=pltpu.CompilerParams(vmem_limit_bytes=32 << 20),
        cost_estimate=cost,
    )(*args)


def on_device(queries, key_states, value_states, layer_grad, out_weight, chosen):
    scale = HD ** (-0.5)
    query, key, value, layer = queries[0], key_states[0], value_states[0], layer_grad[0]
    tokens, width = query.shape
    clips = 4
    cut = layer.shape[1] // clips
    ctx = lax.axis_index("ctx")
    clip = lax.axis_index("clip")
    core = lax.axis_index("head") % 2
    meta = jnp.concatenate(
        [chosen.reshape(-1), jnp.stack([ctx // SIDE, ctx % SIDE, core]).astype(jnp.int32)]
    )

    def to_clip(v, by):
        return lax.ppermute(v, "clip", [(i, (i + by) % clips) for i in range(clips)])

    halves = []
    for d in range(1, clips):
        start = (core * CUBE, lax.rem(clip + d, clips) * cut)
        halves.append(to_clip(lax.dynamic_slice(layer, start, (CUBE, cut)), d))
    key_row, value_row = row_of(key, "x"), row_of(value, "y")
    keys = [key_row, *ends(key_row, "y")]
    values = [value_row, *ends(value_row, "x")]
    near = (*keys[1:], *values[1:])
    keys += far(*near[:2], "y")
    values += far(*near[2:], "x")
    own = lax.dynamic_slice_in_dim(layer, clip * cut, cut, axis=1)
    halves = jnp.stack(lax.optimization_barrier((*halves, key_row, value_row))[: clips - 1])
    there = lax.ppermute(halves, "head", [(h, h ^ 1) for h in range(4)])
    others = jnp.stack([halves, there], axis=1).reshape(-1, cut)
    first = dot(own, out_weight, NT)
    partial = dot(others, out_weight, NT).astype(BF16).reshape(clips - 1, 2, CUBE, width)
    grads = [to_clip(partial[d - 1], -d) for d in range(1, clips)]
    grads = lax.optimization_barrier((*grads, *keys[3:], *values[3:]))[: clips - 1]
    grad = sum(z.astype(F32) for z in grads)
    swap = core * CUBE
    grad = lax.dynamic_slice_in_dim(
        jnp.concatenate([grad[0], grad[1], grad[0]]), swap, tokens, axis=0
    )
    grad = (first + grad).astype(BF16)
    query_row = row_of(after(query, *near), "x")
    grad_ends = ends(grad, "y")
    blocks = SIDE * SIDE
    att, rel, dq, stat, kc, vc = local_call(
        functools.partial(query_kernel, scale),
        [
            (tokens, width),
            (2, CUBE, width),
            (tokens, width),
            (STAT // 2, 2 * width),
            (32, width),
            (32, width),
        ],
        [meta, after(query, query_row, *grad_ends), grad, *blocks_of(keys, tokens), *blocks_of(values, tokens)],
        lambda n: n >= 3,
        [
            pltpu.VMEM((blocks, tokens, width), BF16),
            pltpu.VMEM((blocks, tokens, width), BF16),
            pltpu.SemaphoreType.DMA((5,)),
            pltpu.SemaphoreType.DMA((5,)),
        ],
        pl.CostEstimate(flops=1 << 32, transcendentals=1 << 18, bytes_accessed=6 << 20),
    )
    grad_row = join([grad, *grad_ends, shift(grad, "y", 2)])
    away = [to_clip(rel, d).reshape(tokens, width) for d in range(1, clips)]
    *away, grad_row, query_row = lax.optimization_barrier((*away, grad_row, query_row))
    atts = jnp.concatenate([att, *away], axis=0)
    columns = jnp.concatenate([own, others], axis=0)
    term = lax.dot_general(atts, columns, (((0,), (0,)), ((), ())), preferred_element_type=F32)
    term = term.astype(BF16).reshape(blocks, -1, cut)
    queries_all = [query_row, *ends(query_row, "y")]
    grads_all = [grad_row, *ends(grad_row, "x")]
    term = after(term, *queries_all[1:], *grads_all[1:])
    stats = jnp.broadcast_to(stat[None], (blocks, *stat.shape))
    terms = lax.all_to_all(jnp.concatenate([term, stats], axis=1), "ctx", 0, 0, tiled=True)
    queries_all += far(*queries_all[1:], "y")
    grads_all += far(*grads_all[1:], "x")
    terms = after(terms, *queries_all[3:], *grads_all[3:])
    rows = term.shape[1]
    total = jnp.sum(terms[:, :rows].astype(F32), axis=0).astype(BF16)
    dk, dv = local_call(
        functools.partial(key_kernel, scale),
        [(tokens, width), (tokens, width)],
        [
            meta,
            terms[:, rows:],
            after(key, total),
            value,
            kc,
            vc,
            *blocks_of(queries_all, tokens),
            *blocks_of(grads_all, tokens),
        ],
        lambda n: n >= 6,
        [
            pltpu.VMEM((blocks, tokens, width), BF16),
            pltpu.VMEM((blocks, tokens, width), BF16),
            pltpu.SemaphoreType.DMA((5,)),
            pltpu.SemaphoreType.DMA((5,)),
        ],
        pl.CostEstimate(flops=1 << 33, transcendentals=1 << 21, bytes_accessed=6 << 20),
    )
    copies = jnp.broadcast_to(total[None], (blocks, *total.shape))
    weight = lax.all_to_all(copies, "ctx", 0, 0, tiled=True)
    weight, dk, dv = lax.optimization_barrier((weight, dk, dv))
    return att[None], dq[None], dk[None], dv[None], weight.reshape(width, cut)


def solution(mesh):
    assert mesh.shape["ctx"] == SIDE * SIDE and mesh.shape["clip"] == 4
    tokens = P("clip", "ctx", "head")
    layer = P("clip", "ctx", None)
    weight = P("head", "clip")
    return jax.shard_map(
        on_device,
        mesh=mesh,
        in_specs=(tokens, tokens, tokens, layer, weight, layer),
        out_specs=(tokens, tokens, tokens, tokens, weight),
        check_vma=False,
    )
```
